32 devices in a mesh: blk: 8 (over z, y), grp: 4 (over x, core).
Axes of the slice: x: 2, y: 2, z: 4, core: 2. Of those that a mesh axis runs over, the one named last changes fastest.
Arguments:
- image_features: bfloat16 [4096, 1536], P(('blk', 'grp')), may hold values from -6 to 6
- text_features: bfloat16 [4096, 1024], P(('blk', 'grp')), may hold values from -6 to 6
- image_gain: float32 [1536], replicated, may hold values from 0.25 to 1.75
- text_gain: float32 [1024], replicated, may hold values from 0.25 to 1.75
- image_weight: bfloat16 [1536, 1152], replicated, may hold values from -0.25 to 0.25
- text_weight: bfloat16 [1024, 1152], replicated, may hold values from -0.25 to 0.25
- log_scale: float32 [1], replicated, may hold values from 4.2 to 4.6
- logit_bias: float32 [1], replicated, may hold values from -13 to -9
Outputs:
- loss: float32 [1], replicated
- grad_log_scale: float32 [1], replicated
- grad_bias: float32 [1], replicated
- grad_image_features: bfloat16 [4096, 1536], P(('blk', 'grp'))
- grad_text_features: bfloat16 [4096, 1024], P(('blk', 'grp'))
- grad_image_weight: float32 [1536, 1152], P(('blk', 'grp'))
- grad_text_weight: float32 [1024, 1152], P(('blk', 'grp'))
- grad_image_gain: float32 [1536], replicated
- grad_text_gain: float32 [1024], replicated
The draws below stay inside these ranges and needn't reach their ends.
All inputs are finite; a program needn't handle non-finite values.
Results may differ from the reference program's by a relative error of at most 0.0089.
Values may be sent and summed in bfloat16 or wider, within the bound.
No kernel may reach another device: no remote copies, remote signals or barrier semaphores. Data moves between devices by JAX's collectives and lax.ppermute only.
A program may use at most 128 MiB of HBM per device.

```python
import math
import jax
import jax.numpy as jnp
from jax import lax

DI = 1536
DT = 1024
E = 1152
B_DEV = 128
B_GRP = 1024
B_TOT = 4096
N_BLK = 8
N_GRP = 4


def head_matrix(key, width, salt):
    return jax.random.normal(jax.random.fold_in(key, salt), (width, E), jnp.float32) / math.sqrt(width)


def shared_latent(key):
    clusters = max(B_TOT // 8, 1)
    member = jax.random.randint(jax.random.fold_in(key, 13), (B_TOT,), 0, clusters)
    centres = jax.random.normal(jax.random.fold_in(key, 14), (clusters, E), jnp.float32)
    own = jax.random.normal(jax.random.fold_in(key, 15), (B_TOT, E), jnp.float32)
    strength = 0.6
    return (own + strength * centres[member]) / math.sqrt(1.0 + strength * strength)


def paired_rows(key, width, salt):
    latent = shared_latent(key)
    matrix = head_matrix(key, width, salt)
    signal = jnp.dot(latent, matrix.T, precision=lax.Precision.HIGHEST) / math.sqrt(E / width)
    share = jax.random.uniform(jax.random.fold_in(key, salt + 1), (B_TOT, 1), jnp.float32, 0.5, 0.95)
    noise = jax.random.normal(jax.random.fold_in(key, salt + 2), (B_TOT, width), jnp.float32)
    mixed = share * signal + jnp.sqrt(1.0 - share * share) * noise
    return jnp.clip(mixed, -6.0, 6.0).astype(jnp.bfloat16)


def draw_image_features(key, part):
    return paired_rows(key, DI, 21)


def draw_text_features(key, part):
    return paired_rows(key, DT, 31)


def draw_image_weight(key, part):
    return jnp.clip(head_matrix(key, DI, 21), -0.25, 0.25).astype(jnp.bfloat16)


def draw_text_weight(key, part):
    return jnp.clip(head_matrix(key, DT, 31), -0.25, 0.25).astype(jnp.bfloat16)


def setup_inputs(seed: int = 0) -> dict:
    keys = jax.random.split(jax.random.key(seed), 9)
    image_features = draw_image_features(jax.random.fold_in(keys[8], 71), 0)
    text_features = draw_text_features(jax.random.fold_in(keys[8], 71), 0)
    image_gain = jnp.clip(1.0 + 0.15 * jax.random.normal(keys[2], (DI,), jnp.float32), 0.25, 1.75)
    text_gain = jnp.clip(1.0 + 0.15 * jax.random.normal(keys[3], (DT,), jnp.float32), 0.25, 1.75)
    image_weight = draw_image_weight(jax.random.fold_in(keys[8], 71), 0)
    text_weight = draw_text_weight(jax.random.fold_in(keys[8], 71), 0)
    log_scale = jnp.clip(jax.random.uniform(keys[6], (1,), jnp.float32, 4.2, 4.6), 4.2, 4.6)
    logit_bias = jnp.clip(jax.random.uniform(keys[7], (1,), jnp.float32, -13.0, -9.0), -13.0, -9.0)
    return {"image_features": image_features, "text_features": text_features, "image_gain": image_gain, "text_gain": text_gain, "image_weight": image_weight, "text_weight": text_weight, "log_scale": log_scale, "logit_bias": logit_bias}


def tower_forward(feature, gain, weight):
    xf = feature.astype(jnp.float32)
    center = xf - lax.optimization_barrier(jnp.mean(xf, axis=-1, keepdims=True))
    inv = lax.rsqrt(lax.optimization_barrier(jnp.mean(center * center, axis=-1, keepdims=True)) + 1e-06)
    nhat = center * inv
    hidden = (nhat * gain).astype(jnp.bfloat16)
    proj = jnp.dot(hidden, weight, preferred_element_type=jnp.float32)
    inv_n = lax.rsqrt(lax.optimization_barrier(jnp.sum(proj * proj, axis=-1, keepdims=True)) + 1e-06)
    unit = proj * inv_n
    return (unit.astype(jnp.bfloat16), (nhat, inv, hidden, unit, inv_n))

def tower_backward(d_unit, saved, gain, weight):
    nhat, inv, hidden, unit, inv_n = saved
    d_proj = (d_unit - unit * lax.optimization_barrier(jnp.sum(unit * d_unit, axis=-1, keepdims=True))) * inv_n
    d_projb = d_proj.astype(jnp.bfloat16)
    d_weight = jnp.dot(hidden.T, d_projb, preferred_element_type=jnp.float32)
    d_hidden = jnp.dot(d_projb, weight.T, preferred_element_type=jnp.float32)
    d_nhat = d_hidden * gain
    d_gain = lax.optimization_barrier(jnp.sum(d_hidden * nhat, axis=0))
    d_feature = inv * (d_nhat - lax.optimization_barrier(jnp.mean(d_nhat, axis=-1, keepdims=True)) - nhat * lax.optimization_barrier(jnp.mean(d_nhat * nhat, axis=-1, keepdims=True)))
    return (d_feature.astype(jnp.bfloat16), d_weight, d_gain)

def pair_terms(rows_u, cols_v, row_start, col_start, scale, bias):
    dots = jnp.dot(rows_u, cols_v.T, preferred_element_type=jnp.float32)
    row_ids = row_start + jnp.arange(rows_u.shape[0], dtype=jnp.int32)
    col_ids = col_start + jnp.arange(cols_v.shape[0], dtype=jnp.int32)
    same = row_ids[:, None] == col_ids[None, :]
    sign = jnp.where(same, jnp.float32(1.0), jnp.float32(-1.0))
    logits = scale * dots + bias
    part_loss = -jnp.sum(jax.nn.log_sigmoid(sign * logits))
    grad_logit = -sign * jax.nn.sigmoid(-sign * logits)
    coef = (scale * grad_logit).astype(jnp.bfloat16)
    return (part_loss, scale * jnp.sum(grad_logit * dots), jnp.sum(grad_logit), coef)

def group_pairs(u_group, v_group, scale, bias):
    blocks = u_group.reshape(N_BLK, B_DEV, E)

    def step(carry, item):
        d_text, loss_sum, scale_sum, bias_sum = carry
        block, index = item
        start = (index * B_DEV).astype(jnp.int32)
        part_loss, part_scale, part_bias, coef = pair_terms(block, v_group, start, jnp.int32(0), scale, bias)
        d_block = jnp.dot(coef, v_group, preferred_element_type=jnp.float32)
        d_text = d_text + jnp.dot(coef.T, block, preferred_element_type=jnp.float32)
        return ((d_text, loss_sum + part_loss, scale_sum + part_scale, bias_sum + part_bias), d_block)
    zero = jnp.zeros((), jnp.float32)
    init = (jnp.zeros((B_GRP, E), jnp.float32), zero, zero, zero)
    (d_text, loss_sum, scale_sum, bias_sum), d_image = lax.scan(step, init, (blocks, jnp.arange(N_BLK, dtype=jnp.int32)))
    return (d_image, d_text.reshape(N_BLK, B_DEV, E), loss_sum, scale_sum, bias_sum)

def reference(image_features, text_features, image_gain, text_gain, image_weight, text_weight, log_scale, logit_bias):
    u_emb, saved_image = tower_forward(image_features, image_gain, image_weight)
    v_emb, saved_text = tower_forward(text_features, text_gain, text_weight)
    scale = jnp.exp(log_scale[0])
    bias = logit_bias[0]
    u_split = u_emb.reshape(N_BLK, N_GRP, B_DEV, E)
    v_split = v_emb.reshape(N_BLK, N_GRP, B_DEV, E)
    image_parts = []
    text_parts = []
    loss_sum = jnp.zeros((), jnp.float32)
    scale_sum = jnp.zeros((), jnp.float32)
    bias_sum = jnp.zeros((), jnp.float32)
    for group in range(N_GRP):
        d_image, d_text, part_loss, part_scale, part_bias = group_pairs(u_split[:, group].reshape(B_GRP, E), v_split[:, group].reshape(B_GRP, E), scale, bias)
        image_parts.append(d_image)
        text_parts.append(d_text)
        loss_sum = loss_sum + part_loss
        scale_sum = scale_sum + part_scale
        bias_sum = bias_sum + part_bias
    d_image = jnp.stack(image_parts, axis=1).reshape(B_TOT, E)
    d_text = jnp.stack(text_parts, axis=1).reshape(B_TOT, E)
    gi_feat, gi_weight, gi_gain = tower_backward(d_image, saved_image, image_gain, image_weight)
    gt_feat, gt_weight, gt_gain = tower_backward(d_text, saved_text, text_gain, text_weight)
    return ((loss_sum / B_TOT).reshape(1), scale_sum.reshape(1), bias_sum.reshape(1), gi_feat, gt_feat, gi_weight, gt_weight, gi_gain, gt_gain)
```

```python
import functools

import jax
import jax.numpy as jnp
from jax import lax
from jax.experimental import pallas as pl
from jax.experimental.pallas import tpu as pltpu
from jax.sharding import PartitionSpec as P


F32 = jnp.float32
BF16 = jnp.bfloat16
AXES = ("blk", "grp")
QUAD = 4
VMEM = pl.BlockSpec(memory_space=pltpu.VMEM)
SMEM = pl.BlockSpec(memory_space=pltpu.SMEM)


def cost(flops, nbytes, trans=0):
    return pl.CostEstimate(flops=int(flops), bytes_accessed=int(nbytes), transcendentals=int(trans))


def dot_nt(a, b):
    return lax.dot_general(a, b, (((1,), (1,)), ((), ())), preferred_element_type=F32)


def dot_tn(a, b):
    return lax.dot_general(a, b, (((0,), (0,)), ((), ())), preferred_element_type=F32)


def forward_kernel(x_ref, gain_ref, w_ref, emb_ref, unit_ref, ht_ref, stat_ref, h_ref, acc_ref):
    k = pl.program_id(0)
    depth = w_ref.shape[0]
    lane = lax.broadcasted_iota(jnp.int32, stat_ref.shape, 1)

    @pl.when(k == 0)
    def _():
        xf = x_ref[...].astype(F32)
        mean = jnp.mean(xf, axis=-1, keepdims=True)
        center = xf - mean
        inv = lax.rsqrt(jnp.mean(center * center, axis=-1, keepdims=True) + 1e-06)
        h = (center * inv * gain_ref[...]).astype(BF16)
        h_ref[...] = h
        ht_ref[...] = h.T
        stat_ref[...] = jnp.where(lane == 0, mean, inv)
        acc_ref[...] = jnp.zeros_like(acc_ref)

    part = h_ref[:, pl.ds(pl.multiple_of(k * depth, 128), depth)]
    acc_ref[...] += jnp.dot(part, w_ref[...], preferred_element_type=F32)

    @pl.when(k == pl.num_programs(0) - 1)
    def _():
        proj = acc_ref[...]
        inv_n = lax.rsqrt(jnp.sum(proj * proj, axis=-1, keepdims=True) + 1e-06)
        unit = proj * inv_n
        unit_ref[...] = unit
        emb_ref[...] = unit.astype(BF16)
        stat_ref[...] = jnp.where(lane == 2, inv_n, stat_ref[...])


def tower_forward(x, gain, w, steps):
    rows, width = x.shape
    emb = w.shape[1]
    depth = width // steps
    return pl.pallas_call(
        forward_kernel,
        name="forward",
        grid=(steps,),
        in_specs=[
            pl.BlockSpec((rows, width), lambda k: (0, 0)),
            pl.BlockSpec((1, width), lambda k: (0, 0)),
            pl.BlockSpec((depth, emb), lambda k: (k, 0)),
        ],
        out_specs=[
            pl.BlockSpec((rows, emb), lambda k: (0, 0)),
            pl.BlockSpec((rows, emb), lambda k: (0, 0)),
            pl.BlockSpec((width, rows), lambda k: (0, 0)),
            pl.BlockSpec((rows, 128), lambda k: (0, 0)),
        ],
        out_shape=[
            jax.ShapeDtypeStruct((rows, emb), BF16),
            jax.ShapeDtypeStruct((rows, emb), F32),
            jax.ShapeDtypeStruct((width, rows), BF16),
            jax.ShapeDtypeStruct((rows, 128), F32),
        ],
        scratch_shapes=[pltpu.VMEM((rows, width), BF16), pltpu.VMEM((rows, emb), F32)],
        cost_estimate=cost(2 * rows * width * emb, 2 * width * emb + 8 * rows * width),
    )(x, gain.reshape(1, width), w)


def pair_kernel(n_u, n_v, *refs):
    log_ref, bias_ref = refs[:2]
    u_refs = refs[2 : 2 + n_u]
    v_refs = refs[2 + n_u : 2 + n_u + n_v]
    rest = refs[2 + n_u + n_v :]
    du_refs = rest[:n_u]
    dv_refs = rest[n_u : n_u + n_v]
    sum_ref, u_all, v_all, dv_acc = rest[n_u + n_v :]
    rows = u_refs[0].shape[0]
    scale = jnp.exp(jnp.full((1, 1), log_ref[0], F32))
    bias = bias_ref[0]
    for q in range(n_v):
        v_all[q * rows : (q + 1) * rows, :] = v_refs[q][...]
    step = 2
    totals = [jnp.zeros((1, 1), F32)] * 3
    for base in range(0, n_u, step):
        for i in range(step):
            u_all[i * rows : (i + 1) * rows, :] = u_refs[base + i][...]
        dots = dot_nt(u_all[...], v_all[...])
        logits = scale * dots + bias
        if base == 0:
            row = lax.broadcasted_iota(jnp.int32, dots.shape, 0)
            col = lax.broadcasted_iota(jnp.int32, dots.shape, 1)
            same = (row == col) & (row < rows)
            arg = jnp.where(same, -logits, logits)
        else:
            arg = logits
        e = jnp.exp(-jnp.abs(arg))
        loss = jnp.maximum(arg, 0.0) + jnp.log1p(e)
        r = 1.0 / (1.0 + e)
        g = jnp.where(arg >= 0, r, e * r)
        if base == 0:
            g = jnp.where(same, -g, g)
        full = lambda t: jnp.sum(jnp.sum(t, axis=1, keepdims=True), axis=0, keepdims=True)
        totals = [a + full(t) for a, t in zip(totals, (loss, g * dots, g))]
        coef = (scale * g).astype(BF16)
        du = jnp.dot(coef, v_all[...], preferred_element_type=F32)
        for i in range(step):
            ref = du_refs[base + i]
            ref[...] = du[i * rows : (i + 1) * rows, :].astype(ref.dtype)
        dv = dot_tn(coef, u_all[...])
        if base:
            dv = dv_acc[...] + dv
        if base + step < n_u:
            dv_acc[...] = dv
    for q in range(n_v):
        ref = dv_refs[q]
        ref[...] = dv[q * rows : (q + 1) * rows, :].astype(ref.dtype)
    lane = lax.broadcasted_iota(jnp.int32, sum_ref.shape, 1)
    loss, by_dot, by_bias = totals
    sum_ref[...] = jnp.where(
        lane == 0, loss, jnp.where(lane == 1, scale * by_dot, jnp.where(lane == 2, by_bias, 0.0))
    )


def pair_block(us, vs, log_scale, bias):
    rows, emb = us[0].shape
    n_u, n_v = len(us), len(vs)
    out = lambda n: [jax.ShapeDtypeStruct((rows, emb), F32 if i == 0 else BF16) for i in range(n)]
    got = pl.pallas_call(
        functools.partial(pair_kernel, n_u, n_v),
        name="pairs",
        in_specs=[SMEM, SMEM] + [VMEM] * (n_u + n_v),
        out_specs=[VMEM] * (n_u + n_v + 1),
        out_shape=out(n_u) + out(n_v) + [jax.ShapeDtypeStruct((1, 128), F32)],
        scratch_shapes=[
            pltpu.VMEM((2 * rows, emb), BF16),
            pltpu.VMEM((n_v * rows, emb), BF16),
            pltpu.VMEM((n_v * rows, emb), F32),
        ],
        cost_estimate=cost(6 * n_u * n_v * rows * rows * emb, 10 * (n_u + n_v) * rows * emb),
    )(log_scale, bias, *us, *vs)
    return got[:n_u], got[n_u : n_u + n_v], got[-1]


def project_kernel(n, own_ref, *refs):
    parts, (unit_ref, stat_ref, out_ref) = refs[:n], refs[n:]
    d = own_ref[...]
    for ref in parts:
        d = d + ref[...].astype(F32)
    unit = unit_ref[...]
    along = jnp.sum(unit * d, axis=-1, keepdims=True)
    out_ref[...] = ((d - unit * along) * stat_ref[:, 2:3]).astype(BF16)


def project_back(own, parts, unit, stat):
    rows, emb = own.shape
    return pl.pallas_call(
        functools.partial(project_kernel, len(parts)),
        name="project",
        in_specs=[VMEM] * (3 + len(parts)),
        out_specs=VMEM,
        out_shape=jax.ShapeDtypeStruct((rows, emb), BF16),
        cost_estimate=cost(10 * rows * emb, 14 * rows * emb),
    )(own, *parts, unit, stat)


def weight_kernel(n_blk, first, count, chunk, index_ref, *refs):
    n = QUAD
    ht_refs, dz_refs = refs[:n], refs[n : 2 * n]
    outs = refs[2 * n : -3]
    lhs, rhs, acc = refs[-3:]
    rows = dz_refs[0].shape[0]
    for s in range(n):
        lhs[:, s * rows : (s + 1) * rows] = ht_refs[s][first : first + count, :]
        rhs[s * rows : (s + 1) * rows, :] = dz_refs[s][...]
    if len(outs) == 1:
        outs[0][...] = jnp.dot(lhs[...], rhs[...], preferred_element_type=F32)
        return
    acc[...] = jnp.dot(lhs[...], rhs[...], preferred_element_type=F32)
    blk = index_ref[0]
    for q in range(QUAD):
        for h in range(n_blk // QUAD):
            at = pl.multiple_of((blk ^ (q + QUAD * h)) * chunk, chunk)
            outs[q][h * chunk : (h + 1) * chunk, :] = acc[pl.ds(at, chunk), :].astype(outs[q].dtype)


def weight_grad(hts, dzs, index, n_blk, first, chunk):
    rows, emb = dzs[0].shape
    count = n_blk * chunk
    far = n_blk // QUAD
    aligned = chunk % 16 == 0
    if aligned:
        shapes = [jax.ShapeDtypeStruct((far * chunk, emb), F32 if q == 0 else BF16) for q in range(QUAD)]
    else:
        shapes = [jax.ShapeDtypeStruct((count, emb), F32)]
    got = pl.pallas_call(
        functools.partial(weight_kernel, n_blk, first, count, chunk),
        name="weight",
        in_specs=[SMEM] + [VMEM] * (2 * QUAD),
        out_specs=[VMEM] * len(shapes),
        out_shape=shapes,
        scratch_shapes=[
            pltpu.VMEM((count, QUAD * rows), BF16),
            pltpu.VMEM((QUAD * rows, emb), BF16),
            pltpu.VMEM((count, emb), F32),
        ],
        cost_estimate=cost(2 * QUAD * rows * count * emb, 10 * count * emb),
    )(index, *hts, *dzs)
    if aligned:
        return got
    whole = got[0].reshape(n_blk, chunk, emb)
    picks = []
    for q in range(QUAD):
        ids = index[0] ^ (q + QUAD * jnp.arange(far, dtype=jnp.int32))
        part = jnp.take(whole, ids, axis=0).reshape(far * chunk, emb)
        picks.append(part if q == 0 else part.astype(BF16))
    return picks


def backward_kernel(dz_ref, w_ref, x_ref, gain_ref, stat_ref, df_ref, dg_ref, dh_ref):
    k = pl.program_id(0)
    depth = w_ref.shape[0]
    dh_ref[:, pl.ds(pl.multiple_of(k * depth, 128), depth)] = dot_nt(dz_ref[...], w_ref[...])

    @pl.when(k == pl.num_programs(0) - 1)
    def _():
        mean = stat_ref[:, 0:1]
        inv = stat_ref[:, 1:2]
        nhat = (x_ref[...].astype(F32) - mean) * inv
        dh = dh_ref[...]
        dg_ref[...] = jnp.sum(dh * nhat, axis=0, keepdims=True)
        dn = dh * gain_ref[...]
        m1 = jnp.mean(dn, axis=-1, keepdims=True)
        m2 = jnp.mean(dn * nhat, axis=-1, keepdims=True)
        df_ref[...] = (inv * (dn - m1 - nhat * m2)).astype(BF16)


def tower_backward(dz, w, x, gain, stat, steps):
    rows, width = x.shape
    emb = w.shape[1]
    depth = width // steps
    return pl.pallas_call(
        backward_kernel,
        name="backward",
        grid=(steps,),
        in_specs=[
            pl.BlockSpec((rows, emb), lambda k: (0, 0)),
            pl.BlockSpec((depth, emb), lambda k: (k, 0)),
            pl.BlockSpec((rows, width), lambda k: (0, 0)),
            pl.BlockSpec((1, width), lambda k: (0, 0)),
            pl.BlockSpec((rows, 128), lambda k: (0, 0)),
        ],
        out_specs=[
            pl.BlockSpec((rows, width), lambda k: (0, 0)),
            pl.BlockSpec((1, width), lambda k: (0, 0)),
        ],
        out_shape=[
            jax.ShapeDtypeStruct((rows, width), BF16),
            jax.ShapeDtypeStruct((1, width), F32),
        ],
        scratch_shapes=[pltpu.VMEM((rows, width), F32)],
        cost_estimate=cost(2 * rows * width * emb, 2 * width * emb + 8 * rows * width),
    )(dz, w, x, gain.reshape(1, width), stat)


def make_local(n_blk, n_grp):
    far = n_blk // QUAD

    def swap(x, blk=0, grp=0):
        pairs = [
            (b * n_grp + g, (b ^ blk) * n_grp + (g ^ grp)) for b in range(n_blk) for g in range(n_grp)
        ]
        return lax.ppermute(x, AXES, pairs)

    def local(x_i, x_t, gain_i, gain_t, w_i, w_t, log_scale, bias):
        rows = x_i.shape[0]
        emb = w_i.shape[1]
        size = n_blk * n_grp
        width_i, width_t = x_i.shape[1], x_t.shape[1]
        chunk_i, chunk_t = width_i // size, width_t // size
        blk = lax.axis_index("blk").astype(jnp.int32)
        grp = lax.axis_index("grp").astype(jnp.int32)
        index = blk.reshape(1)

        v, unit_t, ht_t, stat_t = tower_forward(x_t, gain_t, w_t, 4)
        vs = [v] + [swap(v, blk=q) for q in (3, 2, 1)]
        u, unit_i, ht_i, stat_i = tower_forward(x_i, gain_i, w_i, 4)
        us = [u] + [swap(u, blk=QUAD * h) for h in range(1, far)]

        ht_i = ht_i.reshape(n_blk, n_grp, chunk_i, rows)
        ht_t = ht_t.reshape(n_blk, n_grp, chunk_t, rows)
        hts = []
        for s in range(n_grp):
            pick = lambda a: lax.dynamic_index_in_dim(a, grp ^ s, 1, keepdims=False).reshape(-1, rows)
            part = jnp.concatenate([pick(ht_i), pick(ht_t)], axis=0)
            hts.append(swap(part, grp=s) if s else part)

        dus, dvs, sums = pair_block(us, vs, log_scale, bias)
        vs_order = (3, 2, 1)
        du_got = [swap(dus[h], blk=QUAD * h) for h in range(1, far)]
        dv_got = [swap(dvs[1 + i], blk=q) for i, q in enumerate(vs_order)]

        def finish(own, got, unit, stat, first, chunk):
            dz = project_back(own, got, unit, stat)
            dz_x = swap(dz, grp=2)
            dz_c = swap(dz, grp=1)
            dz_xc = swap(dz_x, grp=1)
            parts = weight_grad(hts, [dz, dz_c, dz_x, dz_xc], index, n_blk, first, chunk)
            total = parts[0]
            for q in (3, 2, 1):
                total = total + swap(parts[q], blk=q).astype(F32)
            out = total[:chunk]
            for h in range(1, far):
                out = out + swap(total[h * chunk : (h + 1) * chunk].astype(BF16), blk=QUAD * h).astype(F32)
            return dz, out

        dz_i, grad_wi = finish(dus[0], du_got, unit_i, stat_i, 0, chunk_i)
        dz_t, grad_wt = finish(dvs[0], dv_got, unit_t, stat_t, n_blk * chunk_i, chunk_t)
        df_i, dg_i = tower_backward(dz_i, w_i, x_i, gain_i, stat_i, 4)
        df_t, dg_t = tower_backward(dz_t, w_t, x_t, gain_t, stat_t, 4)

        vec = jnp.concatenate([dg_i, dg_t, sums], axis=1)
        for g in (1, 2):
            vec = vec + swap(vec, grp=g)
        bit = 1
        while bit < n_blk:
            vec = vec + swap(vec, blk=bit)
            bit *= 2
        vec = vec[0]
        at = width_i + width_t
        return (
            vec[at : at + 1] / (rows * size),
            vec[at + 1 : at + 2],
            vec[at + 2 : at + 3],
            df_i,
            df_t,
            grad_wi,
            grad_wt,
            vec[:width_i],
            vec[width_i:at],
        )

    return local


def solution(mesh):
    n_blk, n_grp = mesh.shape["blk"], mesh.shape["grp"]
    both = P(AXES, None)
    return jax.shard_map(
        make_local(n_blk, n_grp),
        mesh=mesh,
        in_specs=(both, both, P(), P(), P(), P(), P(), P()),
        out_specs=(P(), P(), P(), both, both, both, both, P(), P()),
        check_vma=False,
    )
```
